768 devices in a mesh: cuts: 8 (over x, core), stem: 16 (over y, z_hi), rep: 6 (over z_lo).
Axes of the slice: x: 4, y: 8, z: 12 (z_hi: 2, z_lo: 6; z = z_hi * 6 + z_lo), core: 2. Of those that a mesh axis runs over, the one named last changes fastest.
Arguments:
- stem_slabs: bfloat16 [16, 1728, 1728], P('cuts', 'stem'), may hold values from -6 to 6
- site_first: bfloat16 [16, 1728, 1728], P('cuts', 'rep'), may hold values from -0.15625 to 0.15625
- site_second: bfloat16 [16, 1728, 1728], P('cuts', 'rep'), may hold values from -0.15625 to 0.15625
- environment: bfloat16 [16, 8], P('cuts'), may hold values from -2 to 2
Outputs:
- next_stem: bfloat16 [8, 1728, 1728], P('cuts', 'stem')
The draws below stay inside these ranges and needn't reach their ends.
All inputs are finite; a program needn't handle non-finite values.
Results may differ from the reference program's by a relative error of at most 0.0057.
Values may be sent and summed in bfloat16 or wider, within the bound.
No kernel may reach another device: no remote copies, remote signals or barrier semaphores. Data moves between devices by JAX's collectives and lax.ppermute only.
A program may use at most 32 MiB of HBM per device.

```python
import jax
import jax.numpy as jnp
from jax import lax

W = 1728
SLICES = 16
K_NEW = 8


def strengthened(result, stream_key, source, target, blocks, factor):
    owner, partner = [(jnp.arange(result.shape[axis_at]) // (result.shape[axis_at] // blocks)).reshape([-1 if axis == axis_at else 1 for axis in range(result.ndim)]) for axis_at in (source, target)]
    chosen = jax.random.permutation(stream_key, blocks)[partner]
    strong = (owner == chosen) | (owner == (partner + blocks // 2) % blocks)
    return jnp.where(strong, factor * result, result)


def steps_of(key, dims, pieces, low, largest):
    level, own = 1.0, jax.random.fold_in(key, 6)
    for axis_at, shards_of in pieces:
        heights = jnp.exp(jax.random.uniform(jax.random.fold_in(own, axis_at), (shards_of,), jnp.float32, low / len(pieces), largest / len(pieces)))
        level = level * jnp.repeat(heights, dims[axis_at] // shards_of).reshape([-1 if axis == axis_at else 1 for axis in range(len(dims))])
    return level


def centred(key, extent, width, limit, pieces=(), held_as=jnp.bfloat16):
    result = jax.random.normal(key, extent, jnp.float32) * width
    if len(pieces) > 0:
        result = steps_of(key, extent, pieces, -0.22, 0.18) * result
    return jnp.clip(result, min=-limit, max=limit).astype(held_as)


def bell_draw_with(rng, shape, width, bound, cuts, heavy, kind=jnp.bfloat16):
    array = width * jax.random.normal(rng, shape, jnp.float32)
    if cuts:
        array = array * steps_of(rng, shape, cuts, -0.22, 0.18)
    return jnp.clip(strengthened(array, jax.random.fold_in(rng, 3), *heavy), -bound, bound).astype(kind)


def setup_inputs(seed: int = 0) -> dict:
    key_of = jax.random.split(jax.random.key(seed), 5)
    stem_slabs = centred(key_of[0], (SLICES, W, W), 1.0, 6.0, ((0, 8), (1, 16)))
    site_first = centred(key_of[1], (SLICES, W, W), W ** -0.5, 0.15625, ((0, 8), (1, 6)))
    site_second = centred(key_of[2], (SLICES, W, W), W ** -0.5, 0.15625, ((0, 8), (1, 6)))
    environment = bell_draw_with(key_of[3], (SLICES, K_NEW), SLICES ** -0.5, 2.0, ((0, 8),), (0, 1, 8, 2.0))
    return {"stem_slabs": stem_slabs, "site_first": site_first, "site_second": site_second, "environment": environment}


def contract_slab(slab, first_matrix, second_matrix):
    first = jnp.dot(first_matrix, slab.T, preferred_element_type=jnp.float32).astype(jnp.bfloat16)
    final = jnp.dot(second_matrix, first.T, preferred_element_type=jnp.float32).astype(jnp.bfloat16)
    return final


def reference(stem_slabs, site_first, site_second, environment):
    finals = lax.map(lambda items: contract_slab(items[0], items[1], items[2]), (stem_slabs, site_first, site_second))
    summed = jnp.einsum("ck,cij->kij", environment.astype(jnp.float32), finals.astype(jnp.float32))
    return summed.astype(jnp.bfloat16)
```

```python
import jax
import jax.numpy as jnp
from jax import lax
from jax.sharding import Mesh, PartitionSpec as P


Y, HI, REP = 8, 2, 6


def spread(block, axis, n):
    return lax.all_to_all(
        jnp.broadcast_to(block[None], (n, *block.shape)), axis, 0, 0, tiled=True
    )


def body(stem_slabs, site_first, site_second, environment):
    slices, rows, width = stem_slabs.shape
    share = site_first.shape[1]
    y, hi = lax.axis_index("y"), lax.axis_index("hi")

    columns = lax.dynamic_slice_in_dim(site_second, (HI * y + hi) * rows, rows, 2)
    columns = spread(columns, "rep", REP)
    columns = jnp.moveaxis(columns, 0, 1).reshape(slices, Y, width // Y, rows)
    second = lax.all_to_all(jnp.moveaxis(columns, 1, 0), "y", 0, 0, tiled=True)

    first = jnp.einsum(
        "cil,cjl->cij", site_first, stem_slabs, preferred_element_type=jnp.float32
    ).astype(jnp.bfloat16)
    first = spread(first, "y", Y)

    part = jnp.einsum("yckj,ycij->cki", second, first, preferred_element_type=jnp.float32)
    part = part.reshape(slices, HI, rows, share)
    kept = lax.dynamic_index_in_dim(part, hi, 1, keepdims=False)
    given = lax.dynamic_index_in_dim(part, 1 - hi, 1, keepdims=False).astype(jnp.bfloat16)
    taken = lax.ppermute(given, "hi", [(0, 1), (1, 0)])
    final = kept + taken.astype(jnp.float32)

    terms = jnp.einsum("ck,cij->kij", environment.astype(jnp.float32), final).astype(jnp.bfloat16)
    terms = lax.all_to_all(terms, ("x", "core"), 0, 0, tiled=True)
    closed = jnp.sum(terms.astype(jnp.float32), 0).astype(jnp.bfloat16)
    whole = spread(closed, "rep", REP)
    return jnp.moveaxis(whole, 0, 1).reshape(1, rows, width)


def solution(mesh):
    fine = Mesh(mesh.devices.reshape(4, 2, Y, HI, REP), ("x", "core", "y", "hi", "rep"))
    cuts, stem = ("x", "core"), ("y", "hi")
    placed = (P(cuts, stem, None), P(cuts, "rep", None), P(cuts, "rep", None), P(cuts, None))
    return jax.shard_map(
        body, mesh=fine, in_specs=placed, out_specs=P(cuts, stem, None), check_vma=False
    )
```

```python
import jax
import jax.numpy as jnp
from jax import lax
from jax.sharding import Mesh, PartitionSpec as P


Y, HI, PAIRS, DUO = 8, 2, 3, 2
REP = ("pair", "duo")
F32, BF16 = jnp.float32, jnp.bfloat16


def spread(block, axis, n):
    return lax.all_to_all(
        jnp.broadcast_to(block[None], (n, *block.shape)), axis, 0, 0, tiled=True
    )


def body(stem_slabs, site_first, site_second, environment):
    slices, rows, width = stem_slabs.shape
    share = site_first.shape[1]
    y, hi, duo = lax.axis_index("y"), lax.axis_index("hi"), lax.axis_index("duo")

    columns = lax.dynamic_slice_in_dim(site_second, (HI * y + hi) * rows, rows, 2)
    columns = jnp.broadcast_to(columns[None], (PAIRS, *columns.shape))
    columns = lax.all_to_all(
        columns.reshape(PAIRS * DUO, share, rows), REP, 0, 0, tiled=True
    ).reshape(Y, width // Y, rows)

    first = jnp.einsum(
        "cil,cjl->cij", site_first, stem_slabs, preferred_element_type=F32
    ).astype(BF16)
    kept = lax.dynamic_index_in_dim(first, duo, 0, keepdims=False)
    given = lax.dynamic_index_in_dim(first, 1 - duo, 0, keepdims=False)
    taken = lax.ppermute(given, "duo", [(0, 1), (1, 0)])
    low, high = jnp.where(duo == 0, kept, taken), jnp.where(duo == 0, taken, kept)
    mine = jnp.concatenate([low, high])
    packed = jnp.concatenate(
        [jnp.broadcast_to(mine[None], (Y, *mine.shape)), columns], axis=1
    )
    packed = lax.all_to_all(packed, "y", 0, 0, tiled=True)
    first, second = packed[:, : DUO * share], packed[:, DUO * share :]

    part = jnp.einsum("ykj,yij->ki", second, first, preferred_element_type=F32).astype(BF16)
    part = part.reshape(HI, rows, DUO, share).transpose(0, 2, 1, 3)
    part = lax.all_to_all(
        part.reshape(HI * DUO, rows, share), ("hi", "duo"), 0, 0, tiled=True
    )
    part = part.reshape(HI, DUO, rows, share).astype(F32).sum(0)
    terms = jnp.einsum("ck,cij->kij", environment.astype(F32), part).astype(BF16)
    terms = lax.all_to_all(terms, ("x", "core"), 0, 0, tiled=True)
    closed = jnp.sum(terms.astype(F32), 0).astype(BF16)
    whole = spread(closed, REP, PAIRS * DUO)
    return jnp.moveaxis(whole, 0, 1).reshape(1, rows, width)


def solution(mesh):
    fine = Mesh(
        mesh.devices.reshape(4, 2, Y, HI, PAIRS, DUO), ("x", "core", "y", "hi", *REP)
    )
    cuts, stem = ("x", "core"), ("y", "hi")
    placed = (P(cuts, stem, None), P(cuts, REP, None), P(cuts, REP, None), P(cuts, None))
    return jax.shard_map(
        body, mesh=fine, in_specs=placed, out_specs=P(cuts, stem, None), check_vma=False
    )
```

```python
import jax
import jax.numpy as jnp
from jax import lax
from jax.sharding import Mesh, PartitionSpec as P


Y, HI, PAIRS, DUO = 8, 2, 3, 2
REP = ("pair", "duo")
Z = ("hi", *REP)
F32, BF16 = jnp.float32, jnp.bfloat16


def spread(block, axis, n):
    return lax.all_to_all(
        jnp.broadcast_to(block[None], (n, *block.shape)), axis, 0, 0, tiled=True
    )


def pick(array, index):
    return lax.dynamic_index_in_dim(array, index, 0, keepdims=False)


def body(stem_slabs, site_first, site_second, environment):
    slices, rows, width = stem_slabs.shape
    share = site_first.shape[1]
    n_rep, ring = PAIRS * DUO, HI * PAIRS * DUO
    y, hi, rep, duo = (lax.axis_index(a) for a in ("y", "hi", REP, "duo"))

    columns = lax.dynamic_slice_in_dim(site_second, HI * rows * y, HI * rows, 2)
    even, odd = pick(columns, duo), pick(columns, 1 - duo)
    second = jnp.zeros((n_rep, share, HI * rows), BF16)
    second = lax.dynamic_update_index_in_dim(second, even, rep, 0)
    for step in (1, -1, 2, -2, 3):
        piece = lax.ppermute(
            odd if step % 2 else even, Z, [(i, (i + step) % ring) for i in range(ring)]
        )
        second = lax.dynamic_update_index_in_dim(second, piece, (rep - step) % n_rep, 0)
    second = second.reshape(Y, HI, rows, HI * rows)
    second = lax.dynamic_index_in_dim(second, hi, 1, keepdims=False)

    first = jnp.einsum(
        "cil,cjl->cij", site_first, stem_slabs, preferred_element_type=F32
    ).astype(BF16)
    even, odd = pick(first, duo), pick(first, 1 - duo)
    quad = ("hi", "duo")
    near = lax.ppermute(odd, quad, [(i, i ^ 1) for i in range(HI * DUO)])
    far = lax.ppermute(even, quad, [(i, i ^ 2) for i in range(HI * DUO)])
    both = lax.ppermute(odd, quad, [(i, i ^ 3) for i in range(HI * DUO)])
    own, other = jnp.stack([even, near]), jnp.stack([far, both])
    own, other = jnp.where(duo == 0, own, own[::-1]), jnp.where(duo == 0, other, other[::-1])
    first = jnp.concatenate(
        [jnp.where(hi == 0, own, other), jnp.where(hi == 0, other, own)], axis=2
    )

    part = jnp.einsum("ykj,dij->ydki", second, first, preferred_element_type=F32).astype(BF16)
    part = lax.all_to_all(
        part.reshape(Y * DUO, rows, share), ("y", "duo"), 0, 0, tiled=True
    )
    part = part.reshape(Y, DUO, rows, share).astype(F32).sum(0)
    terms = jnp.einsum("ck,cij->kij", environment.astype(F32), part).astype(BF16)
    terms = lax.all_to_all(terms, ("x", "core"), 0, 0, tiled=True)
    closed = jnp.sum(terms.astype(F32), 0).astype(BF16)
    whole = spread(closed, REP, n_rep)
    return jnp.moveaxis(whole, 0, 1).reshape(1, rows, width)


def solution(mesh):
    fine = Mesh(
        mesh.devices.reshape(4, 2, Y, HI, PAIRS, DUO), ("x", "core", "y", "hi", *REP)
    )
    cuts, stem = ("x", "core"), ("y", "hi")
    placed = (P(cuts, stem, None), P(cuts, REP, None), P(cuts, REP, None), P(cuts, None))
    return jax.shard_map(
        body, mesh=fine, in_specs=placed, out_specs=P(cuts, stem, None), check_vma=False
    )
```

```python
import jax
import jax.numpy as jnp
from jax import lax
from jax.sharding import Mesh, PartitionSpec as P


Y, HI, PAIRS, DUO = 8, 2, 3, 2
REP = ("pair", "duo")
F32, BF16 = jnp.float32, jnp.bfloat16


def spread(block, axis, n):
    return lax.all_to_all(
        jnp.broadcast_to(block[None], (n, *block.shape)), axis, 0, 0, tiled=True
    )


def pick(array, index):
    return lax.dynamic_index_in_dim(array, index, 0, keepdims=False)


def owned_rows(columns, hi, rows, share):
    blocks = {}
    for rep in range(columns.shape[0]):
        at = (rows * hi - share * rep) % (HI * rows)
        pieces = [(at, rows, 0)]
        if at < rows and at + HI * rows < share:
            begin = at + HI * rows
            pieces.append((begin, share - begin, rows + begin - (share - 2 * rows // 3)))
        elif at > rows:
            pieces.append((0, at - rows, rows))
        for begin, count, held in pieces:
            block = blocks.setdefault((share * rep + begin) // (HI * rows), [])
            block.append(columns[rep, held : held + count])
    return jnp.stack([jnp.concatenate(blocks[k]) for k in range(len(blocks))])


def body(stem_slabs, site_first, site_second, environment):
    slices, rows, width = stem_slabs.shape
    share = site_first.shape[1]
    n_rep = PAIRS * DUO
    y, hi, rep, duo = (lax.axis_index(a) for a in ("y", "hi", REP, "duo"))

    extra = 2 * rows // 3
    columns = lax.dynamic_slice_in_dim(site_second, HI * rows * y, HI * rows, 2)
    at = lax.rem(rows * hi + HI * rows * n_rep - share * rep % (HI * rows), HI * rows)
    side = jnp.where(at < rows, share - extra, 0)
    columns = jnp.concatenate(
        [
            lax.dynamic_slice_in_dim(columns, at, rows, 1),
            lax.dynamic_slice_in_dim(columns, side, extra, 1),
        ],
        axis=1,
    )
    columns = jnp.broadcast_to(columns[None], (PAIRS, *columns.shape))
    columns = lax.all_to_all(
        columns.reshape(n_rep, rows + extra, HI * rows), REP, 0, 0, tiled=True
    )
    second = jnp.where(
        hi == 0, owned_rows(columns, 0, rows, share), owned_rows(columns, 1, rows, share)
    )

    first = jnp.einsum(
        "cil,cjl->cij", site_first, stem_slabs, preferred_element_type=F32
    ).astype(BF16)
    even, odd = pick(first, duo), pick(first, 1 - duo)
    near = lax.ppermute(odd, "duo", [(0, 1), (1, 0)])
    own = jnp.concatenate(
        [jnp.where(duo == 0, even, near), jnp.where(duo == 0, near, even)], axis=0
    )
    other = lax.ppermute(own, "hi", [(0, 1), (1, 0)])
    first = jnp.concatenate(
        [jnp.where(hi == 0, own, other), jnp.where(hi == 0, other, own)], axis=1
    ).reshape(DUO, share, HI * rows)

    part = jnp.einsum("ykj,dij->ydki", second, first, preferred_element_type=F32).astype(BF16)
    part = lax.all_to_all(
        part.reshape(Y * DUO, rows, share), ("y", "duo"), 0, 0, tiled=True
    )
    part = part.reshape(Y, DUO, rows, share).astype(F32).sum(0)
    terms = jnp.einsum("ck,cij->kij", environment.astype(F32), part).astype(BF16)
    terms = lax.all_to_all(terms, ("x", "core"), 0, 0, tiled=True)
    closed = jnp.sum(terms.astype(F32), 0).astype(BF16)
    whole = spread(closed, REP, n_rep)
    return jnp.moveaxis(whole, 0, 1).reshape(1, rows, width)


def solution(mesh):
    fine = Mesh(
        mesh.devices.reshape(4, 2, Y, HI, PAIRS, DUO), ("x", "core", "y", "hi", *REP)
    )
    cuts, stem = ("x", "core"), ("y", "hi")
    placed = (P(cuts, stem, None), P(cuts, REP, None), P(cuts, REP, None), P(cuts, None))
    return jax.shard_map(
        body, mesh=fine, in_specs=placed, out_specs=P(cuts, stem, None), check_vma=False
    )
```

```python
import jax
import jax.numpy as jnp
from jax import lax
from jax.experimental import pallas as pl
from jax.experimental.pallas import tpu as pltpu
from jax.sharding import Mesh, PartitionSpec as P


Y, HI, PAIRS, DUO = 8, 2, 3, 2
LANES = 128
REP = ("pair", "duo")
F32, BF16 = jnp.float32, jnp.bfloat16


def spread(block, axis, n):
    return lax.all_to_all(
        jnp.broadcast_to(block[None], (n, *block.shape)), axis, 0, 0, tiled=True
    )


def pick(array, index):
    return lax.dynamic_index_in_dim(array, index, 0, keepdims=False)


def pieces_of(hi, rows, share, n_rep):
    period, found, filled = HI * rows, [], {}
    for rep in range(n_rep):
        at = (rows * hi - share * rep) % period
        parts = [(at, rows, 0)]
        if at < rows and at + period < share:
            begin = at + period
            parts.append((begin, share - begin, rows + begin - (share - 2 * rows // 3)))
        elif at > rows:
            parts.append((0, at - rows, rows))
        for begin, count, held in parts:
            block = (share * rep + begin) // period
            found.append((block, filled.get(block, 0), rep, held, count))
            filled[block] = filled.get(block, 0) + count
    return found


def multiply(hi_ref, columns_ref, first_ref, out_ref, second_ref):
    n_rep, rows = columns_ref.shape[0], second_ref.shape[1]
    share = first_ref.shape[1]
    for side in range(HI):

        @pl.when(hi_ref[0] == side)
        def _():
            for block, row, rep, held, count in pieces_of(side, rows, share, n_rep):
                second_ref[block, row : row + count] = columns_ref[rep, held : held + count]

    whole, rest = share // LANES, share % LANES
    fold = LANES // rest
    deep = rows // fold
    for block in range(second_ref.shape[0]):
        for duo in range(DUO):
            got = lax.dot_general(
                second_ref[block], first_ref[duo], (((1,), (1,)), ((), ())),
                preferred_element_type=F32,
            )
            left = got[:, whole * LANES :]
            packed = [got[:, n * LANES : (n + 1) * LANES] for n in range(whole)]
            packed.append(
                jnp.concatenate([left[n * deep : (n + 1) * deep] for n in range(fold)], axis=1)
            )
            used = whole * rows + deep
            packed.append(jnp.zeros((out_ref.shape[1] - used, LANES), F32))
            out_ref[block * DUO + duo] = jnp.concatenate(packed, axis=0).astype(BF16)


def unpack(packed_ref, out_ref):
    rows = out_ref.shape[0]
    share = out_ref.shape[1] // packed_ref.shape[0]
    whole, rest = share // LANES, share % LANES
    fold = LANES // rest
    deep = rows // fold
    columns = []
    for rep in range(packed_ref.shape[0]):
        held = packed_ref[rep].astype(F32)
        left = held[whole * rows : whole * rows + deep]
        columns += [held[n * rows : (n + 1) * rows] for n in range(whole)]
        columns.append(
            jnp.concatenate([left[:, n * rest : (n + 1) * rest] for n in range(fold)], axis=0)
        )
    out_ref[...] = jnp.concatenate(columns, axis=1).astype(BF16)


def body(stem_slabs, site_first, site_second, environment):
    slices, rows, width = stem_slabs.shape
    share = site_first.shape[1]
    n_rep = PAIRS * DUO
    y, hi, rep, duo = (lax.axis_index(a) for a in ("y", "hi", REP, "duo"))

    first = jnp.einsum(
        "cil,cjl->cij", site_first, stem_slabs, preferred_element_type=F32
    ).astype(BF16)
    even, odd = pick(first, duo), pick(first, 1 - duo)
    site_second, odd = lax.optimization_barrier((site_second, odd))

    extra = 2 * rows // 3
    columns = lax.dynamic_slice_in_dim(site_second, HI * rows * y, HI * rows, 2)
    at = lax.rem(rows * hi + HI * rows * n_rep - share * rep % (HI * rows), HI * rows)
    side = jnp.where(at < rows, share - extra, 0)
    columns = jnp.concatenate(
        [
            lax.dynamic_slice_in_dim(columns, at, rows, 1),
            lax.dynamic_slice_in_dim(columns, side, extra, 1),
        ],
        axis=1,
    )
    columns = jnp.broadcast_to(columns[None], (PAIRS, *columns.shape))
    columns = lax.all_to_all(
        columns.reshape(n_rep, rows + extra, HI * rows), REP, 0, 0, tiled=True
    )
    near = lax.ppermute(odd, "duo", [(0, 1), (1, 0)])
    own = jnp.concatenate(
        [jnp.where(duo == 0, even, near), jnp.where(duo == 0, near, even)], axis=0
    )
    other = lax.ppermute(own, "hi", [(0, 1), (1, 0)])
    first = jnp.concatenate(
        [jnp.where(hi == 0, own, other), jnp.where(hi == 0, other, own)], axis=1
    ).reshape(DUO, share, HI * rows)

    deep = -(-rows * share // LANES // 8) * 8
    vmem = pl.BlockSpec(memory_space=pltpu.VMEM)
    part = pl.pallas_call(
        multiply,
        out_shape=jax.ShapeDtypeStruct((Y * DUO, deep, LANES), BF16),
        in_specs=[pl.BlockSpec(memory_space=pltpu.SMEM), vmem, vmem],
        out_specs=vmem,
        scratch_shapes=[pltpu.VMEM((Y, rows, HI * rows), BF16)],
        compiler_params=pltpu.CompilerParams(vmem_limit_bytes=12 << 20),
    )(hi[None].astype(jnp.int32), columns, first)
    part = lax.all_to_all(part, ("y", "duo"), 0, 0, tiled=True)
    part = part.reshape(Y, DUO, deep, LANES).astype(F32).sum(0)
    weights = environment.astype(F32)[:, :, None, None]
    terms = sum(weights[c] * part[c] for c in range(slices)).astype(BF16)
    terms = lax.all_to_all(terms, ("x", "core"), 0, 0, tiled=True)
    closed = jnp.sum(terms.astype(F32), 0).astype(BF16)
    whole = spread(closed, REP, n_rep)
    return pl.pallas_call(
        unpack,
        out_shape=jax.ShapeDtypeStruct((rows, width), BF16),
        in_specs=[vmem],
        out_specs=vmem,
        compiler_params=pltpu.CompilerParams(vmem_limit_bytes=12 << 20),
    )(whole)[None]


def solution(mesh):
    fine = Mesh(
        mesh.devices.reshape(4, 2, Y, HI, PAIRS, DUO), ("x", "core", "y", "hi", *REP)
    )
    cuts, stem = ("x", "core"), ("y", "hi")
    placed = (P(cuts, stem, None), P(cuts, REP, None), P(cuts, REP, None), P(cuts, None))
    return jax.shard_map(
        body, mesh=fine, in_specs=placed, out_specs=P(cuts, stem, None), check_vma=False
    )
```

```python
import jax
import jax.numpy as jnp
from jax import lax
from jax.experimental import pallas as pl
from jax.experimental.pallas import tpu as pltpu
from jax.sharding import Mesh, PartitionSpec as P


U, V, HI, PAIRS, DUO = 4, 2, 2, 3, 2
LANES = 128
REP = ("pair", "duo")
F32, BF16 = jnp.float32, jnp.bfloat16


def spread(block, axis, n):
    return lax.all_to_all(
        jnp.broadcast_to(block[None], (n, *block.shape)), axis, 0, 0, tiled=True
    )


def pick(array, index):
    return lax.dynamic_index_in_dim(array, index, 0, keepdims=False)


def pieces_of(owner, rows, share, n_rep):
    found = []
    for block in range(U):
        begin, filled = rows * (V * HI * block + owner), 0
        for rep in range(n_rep):
            low, high = max(begin, share * rep), min(begin + rows, share * (rep + 1))
            if low < high:
                window = min(max(begin - share * rep, 0), share - rows)
                found.append((block, filled, rep, low - share * rep - window, high - low))
                filled += high - low
    return found


def folded(value, used):
    rows, lanes = value.shape
    whole, rest = lanes // LANES, lanes % LANES
    fold = LANES // rest
    deep = rows // fold
    left = value[:, whole * LANES :]
    side = [left[n * deep : (n + 1) * deep] for n in range(fold)]
    if fold * rest < LANES:
        side.append(jnp.zeros((deep, LANES - fold * rest), value.dtype))
    packed = [value[:, n * LANES : (n + 1) * LANES] for n in range(whole)]
    packed.append(jnp.concatenate(side, axis=1))
    if used > whole * rows + deep:
        packed.append(jnp.zeros((used - whole * rows - deep, LANES), value.dtype))
    return jnp.concatenate(packed, axis=0)


def unfolded(packed, rows, lanes):
    whole, rest = lanes // LANES, lanes % LANES
    fold = LANES // rest
    left = packed[whole * rows : whole * rows + rows // fold]
    left = jnp.concatenate([left[:, n * rest : (n + 1) * rest] for n in range(fold)], axis=0)
    return jnp.concatenate([packed[n * rows : (n + 1) * rows] for n in range(whole)] + [left], axis=1)


def fold_size(rows, lanes):
    return -(-(lanes // LANES * rows + rows // (LANES // (lanes % LANES))) // 8) * 8


def pack(columns_ref, out_ref):
    for duo in range(DUO):
        packed = folded(columns_ref[duo].astype(F32), out_ref.shape[1]).astype(BF16)
        for pair in range(out_ref.shape[0] // DUO):
            out_ref[pair * DUO + duo] = packed


def multiply(owner_ref, columns_ref, first_ref, out_ref, window_ref, second_ref):
    n_rep = columns_ref.shape[0]
    rows, depth = second_ref.shape[1:]
    share = first_ref.shape[1]
    for rep in range(n_rep):
        window_ref[rep] = unfolded(columns_ref[rep].astype(F32), rows, depth).astype(BF16)
    for owner in range(V * HI):

        @pl.when(owner_ref[0] == owner)
        def _():
            for block, row, rep, held, count in pieces_of(owner, rows, share, n_rep):
                second_ref[block, row : row + count] = window_ref[rep, held : held + count]

    for block in range(second_ref.shape[0]):
        for duo in range(DUO):
            got = lax.dot_general(
                second_ref[block], first_ref[duo], (((1,), (1,)), ((), ())),
                preferred_element_type=F32,
            )
            out_ref[block * DUO + duo] = folded(got, out_ref.shape[1]).astype(BF16)


def unpack(packed_ref, out_ref):
    n_rep, rows = packed_ref.shape[0], out_ref.shape[0]
    share = out_ref.shape[1] // n_rep
    columns = [unfolded(packed_ref[rep].astype(F32), rows, share) for rep in range(n_rep)]
    out_ref[...] = jnp.concatenate(columns, axis=1).astype(BF16)


def body(stem_slabs, site_first, site_second, environment):
    slices, rows, width = stem_slabs.shape
    share = site_first.shape[1]
    n_rep = PAIRS * DUO
    u, v, hi, rep, duo = (lax.axis_index(a) for a in ("u", "v", "hi", REP, "duo"))
    vmem = pl.BlockSpec(memory_space=pltpu.VMEM)
    params = pltpu.CompilerParams(vmem_limit_bytes=12 << 20)

    first = jnp.einsum(
        "cil,cjl->cij", site_first, stem_slabs, preferred_element_type=F32
    ).astype(BF16)
    even, odd = pick(first, duo), pick(first, 1 - duo)
    site_second, odd = lax.optimization_barrier((site_second, odd))

    owner, depth = HI * v + hi, V * HI * rows
    block = lax.div(share * rep + (V * HI - 1) * rows - rows * owner, V * HI * rows)
    window = jnp.clip(rows * (owner + V * HI * block) - share * rep, 0, share - rows)
    columns = lax.dynamic_slice(
        site_second, (0, window, depth * u), (slices, rows, depth)
    )
    columns = pl.pallas_call(
        pack,
        out_shape=jax.ShapeDtypeStruct((n_rep, fold_size(rows, depth), LANES), BF16),
        in_specs=[vmem],
        out_specs=vmem,
        compiler_params=params,
    )(columns)
    columns = lax.all_to_all(columns, REP, 0, 0, tiled=True)
    near = lax.ppermute(odd, "duo", [(0, 1), (1, 0)])
    own = jnp.concatenate(
        [jnp.where(duo == 0, even, near), jnp.where(duo == 0, near, even)], axis=0
    )
    other = lax.ppermute(own, "hi", [(0, 1), (1, 0)])
    own = jnp.concatenate(
        [jnp.where(hi == 0, own, other), jnp.where(hi == 0, other, own)], axis=1
    )
    other = lax.ppermute(own, "v", [(0, 1), (1, 0)])
    first = jnp.concatenate(
        [jnp.where(v == 0, own, other), jnp.where(v == 0, other, own)], axis=1
    ).reshape(DUO, share, depth)

    deep = fold_size(rows, share)
    part = pl.pallas_call(
        multiply,
        out_shape=jax.ShapeDtypeStruct((U * DUO, deep, LANES), BF16),
        in_specs=[pl.BlockSpec(memory_space=pltpu.SMEM), vmem, vmem],
        out_specs=vmem,
        scratch_shapes=[
            pltpu.VMEM((n_rep, rows, depth), BF16),
            pltpu.VMEM((U, rows, depth), BF16),
        ],
        compiler_params=params,
    )(owner[None].astype(jnp.int32), columns, first)
    part = lax.all_to_all(part, ("u", "duo"), 0, 0, tiled=True)
    part = part.reshape(U, DUO, deep, LANES).astype(F32).sum(0)
    weights = environment.astype(F32)[:, :, None, None]
    terms = sum(weights[c] * part[c] for c in range(slices)).astype(BF16)
    terms = lax.all_to_all(terms, ("x", "core"), 0, 0, tiled=True)
    closed = jnp.sum(terms.astype(F32), 0).astype(BF16)
    whole = spread(closed, REP, n_rep)
    return pl.pallas_call(
        unpack,
        out_shape=jax.ShapeDtypeStruct((rows, width), BF16),
        in_specs=[vmem],
        out_specs=vmem,
        compiler_params=params,
    )(whole)[None]


def solution(mesh):
    fine = Mesh(
        mesh.devices.reshape(4, 2, U, V, HI, PAIRS, DUO),
        ("x", "core", "u", "v", "hi", *REP),
    )
    cuts, stem = ("x", "core"), ("u", "v", "hi")
    placed = (P(cuts, stem, None), P(cuts, REP, None), P(cuts, REP, None), P(cuts, None))
    return jax.shard_map(
        body, mesh=fine, in_specs=placed, out_specs=P(cuts, stem, None), check_vma=False
    )
```

```python
import jax
import jax.numpy as jnp
from jax import lax
from jax.experimental import pallas as pl
from jax.experimental.pallas import tpu as pltpu
from jax.sharding import Mesh, PartitionSpec as P


U, V, HI, PAIRS, DUO = 4, 2, 2, 3, 2
LANES = 128
SWAP = [(0, 1), (1, 0)]
REP = ("pair", "duo")
Z = ("hi", *REP)
F32, BF16 = jnp.float32, jnp.bfloat16


def spread(block, axis, n):
    return lax.all_to_all(
        jnp.broadcast_to(block[None], (n, *block.shape)), axis, 0, 0, tiled=True
    )


def pick(array, index):
    return lax.dynamic_index_in_dim(array, index, 0, keepdims=False)


def pieces_of(owner, rows, share, n_rep):
    found = []
    for block in range(U):
        begin, filled = rows * (V * HI * block + owner), 0
        for rep in range(n_rep):
            low, high = max(begin, share * rep), min(begin + rows, share * (rep + 1))
            if low < high:
                window = min(max(begin - share * rep, 0), share - rows)
                found.append((block, filled, rep, low - share * rep - window, high - low))
                filled += high - low
    return found


def folded(value, used):
    rows, lanes = value.shape
    whole, rest = lanes // LANES, lanes % LANES
    fold = LANES // rest
    deep = rows // fold
    left = value[:, whole * LANES :]
    side = [left[n * deep : (n + 1) * deep] for n in range(fold)]
    if fold * rest < LANES:
        side.append(jnp.zeros((deep, LANES - fold * rest), value.dtype))
    packed = [value[:, n * LANES : (n + 1) * LANES] for n in range(whole)]
    packed.append(jnp.concatenate(side, axis=1))
    if used > whole * rows + deep:
        packed.append(jnp.zeros((used - whole * rows - deep, LANES), value.dtype))
    return jnp.concatenate(packed, axis=0)


def unfolded(packed, rows, lanes):
    whole, rest = lanes // LANES, lanes % LANES
    fold = LANES // rest
    left = packed[whole * rows : whole * rows + rows // fold]
    left = jnp.concatenate([left[:, n * rest : (n + 1) * rest] for n in range(fold)], axis=0)
    return jnp.concatenate([packed[n * rows : (n + 1) * rows] for n in range(whole)] + [left], axis=1)


def fold_size(rows, lanes):
    return -(-(lanes // LANES * rows + rows // (LANES // (lanes % LANES))) // 8) * 8


def pack(*refs):
    out_ref = refs[-1]
    for side in range(HI):
        for duo in range(DUO):
            packed = folded(refs[side][duo].astype(F32), out_ref.shape[2])
            out_ref[duo, side] = packed.astype(BF16)


def multiply(where_ref, here_ref, below_ref, above_ref, first_ref, out_ref, window_ref, second_ref):
    n_rep = window_ref.shape[0]
    rows, depth = second_ref.shape[1:]
    share = first_ref.shape[1]
    for place, ref in enumerate((here_ref, below_ref, above_ref)):
        for duo in range(DUO):
            window_ref[DUO * where_ref[1 + place] + duo] = unfolded(
                ref[duo].astype(F32), rows, depth
            ).astype(BF16)
    for owner in range(V * HI):

        @pl.when(where_ref[0] == owner)
        def _():
            for block, row, rep, held, count in pieces_of(owner, rows, share, n_rep):
                second_ref[block, row : row + count] = window_ref[rep, held : held + count]

    for block in range(second_ref.shape[0]):
        for duo in range(DUO):
            got = lax.dot_general(
                second_ref[block], first_ref[duo], (((1,), (1,)), ((), ())),
                preferred_element_type=F32,
            )
            out_ref[block * DUO + duo] = folded(got, out_ref.shape[1]).astype(BF16)


def unpack(packed_ref, out_ref):
    n_rep, rows = packed_ref.shape[0], out_ref.shape[0]
    share = out_ref.shape[1] // n_rep
    columns = [unfolded(packed_ref[rep].astype(F32), rows, share) for rep in range(n_rep)]
    out_ref[...] = jnp.concatenate(columns, axis=1).astype(BF16)


def body(stem_slabs, site_first, site_second, environment):
    slices, rows, width = stem_slabs.shape
    share = site_first.shape[1]
    n_rep = PAIRS * DUO
    u, v, hi, rep, pair, duo = (lax.axis_index(a) for a in ("u", "v", "hi", REP, *REP))
    vmem = pl.BlockSpec(memory_space=pltpu.VMEM)
    params = pltpu.CompilerParams(vmem_limit_bytes=12 << 20)

    first = jnp.einsum(
        "cil,cjl->cij", site_first, stem_slabs, preferred_element_type=F32
    ).astype(BF16)
    even, odd = pick(first, duo), pick(first, 1 - duo)

    depth = V * HI * rows
    windows = []
    for side in range(HI):
        owner = HI * v + side
        block = lax.div(share * rep + (V * HI - 1) * rows - rows * owner, V * HI * rows)
        at = jnp.clip(rows * (owner + V * HI * block) - share * rep, 0, share - rows)
        windows.append(lax.dynamic_slice(site_second, (0, at, depth * u), (slices, rows, depth)))
    windows = pl.pallas_call(
        pack,
        out_shape=jax.ShapeDtypeStruct((DUO, HI, fold_size(rows, depth), LANES), BF16),
        in_specs=[vmem, vmem],
        out_specs=vmem,
        compiler_params=params,
    )(*windows)
    kept = pick(windows, duo)
    taken = lax.ppermute(pick(windows, 1 - duo), "duo", SWAP)
    windows = jnp.stack(
        [jnp.where(duo == 0, kept, taken), jnp.where(duo == 0, taken, kept)], axis=1
    )
    where = [HI * v + hi, pair, (pair + PAIRS - 1) % PAIRS, (pair + 1) % PAIRS]

    near = lax.ppermute(odd, "duo", SWAP)
    own = jnp.concatenate(
        [jnp.where(duo == 0, even, near), jnp.where(duo == 0, near, even)], axis=0
    )
    other = lax.ppermute(own, "hi", SWAP)
    ring = HI * n_rep
    up = jnp.where(pair < PAIRS - 1, hi, 1 - hi)
    down = jnp.where(pair > 0, hi, 1 - hi)
    turn = [(i, (i + DUO) % ring) for i in range(ring)]
    below = lax.ppermute(pick(windows, up), Z, turn)
    above = lax.ppermute(pick(windows, down), Z, [(j, i) for i, j in turn])
    own = jnp.concatenate(
        [jnp.where(hi == 0, own, other), jnp.where(hi == 0, other, own)], axis=1
    )
    other = lax.ppermute(own, "v", SWAP)
    first = jnp.concatenate(
        [jnp.where(v == 0, own, other), jnp.where(v == 0, other, own)], axis=1
    ).reshape(DUO, share, depth)

    deep = fold_size(rows, share)
    part = pl.pallas_call(
        multiply,
        out_shape=jax.ShapeDtypeStruct((U * DUO, deep, LANES), BF16),
        in_specs=[pl.BlockSpec(memory_space=pltpu.SMEM), vmem, vmem, vmem, vmem],
        out_specs=vmem,
        scratch_shapes=[
            pltpu.VMEM((n_rep, rows, depth), BF16),
            pltpu.VMEM((U, rows, depth), BF16),
        ],
        compiler_params=params,
    )(jnp.stack(where).astype(jnp.int32), pick(windows, hi), below, above, first)
    part = lax.all_to_all(part, ("u", "duo"), 0, 0, tiled=True)
    part = part.reshape(U, DUO, deep, LANES).astype(F32).sum(0)
    weights = environment.astype(F32)[:, :, None, None]
    terms = sum(weights[c] * part[c] for c in range(slices)).astype(BF16)
    terms = lax.all_to_all(terms, ("x", "core"), 0, 0, tiled=True)
    closed = jnp.sum(terms.astype(F32), 0).astype(BF16)
    whole = spread(closed, REP, n_rep)
    return pl.pallas_call(
        unpack,
        out_shape=jax.ShapeDtypeStruct((rows, width), BF16),
        in_specs=[vmem],
        out_specs=vmem,
        compiler_params=params,
    )(whole)[None]


def solution(mesh):
    fine = Mesh(
        mesh.devices.reshape(4, 2, U, V, HI, PAIRS, DUO),
        ("x", "core", "u", "v", "hi", *REP),
    )
    cuts, stem = ("x", "core"), ("u", "v", "hi")
    placed = (P(cuts, stem, None), P(cuts, REP, None), P(cuts, REP, None), P(cuts, None))
    return jax.shard_map(
        body, mesh=fine, in_specs=placed, out_specs=P(cuts, stem, None), check_vma=False
    )
```

```python
import jax
import jax.numpy as jnp
from jax import lax
from jax.experimental import pallas as pl
from jax.experimental.pallas import tpu as pltpu
from jax.sharding import Mesh, PartitionSpec as P


U, V, HI, PAIRS, DUO = 4, 2, 2, 3, 2
LANES = 128
SWAP = [(0, 1), (1, 0)]
REP = ("pair", "duo")
Z = ("hi", *REP)
F32, BF16 = jnp.float32, jnp.bfloat16


def spread(block, axis, n):
    return lax.all_to_all(
        jnp.broadcast_to(block[None], (n, *block.shape)), axis, 0, 0, tiled=True
    )


def pick(array, index):
    return lax.dynamic_index_in_dim(array, index, 0, keepdims=False)


def pieces_of(owner, rows, share, n_rep):
    found = []
    for block in range(U):
        begin, filled = rows * (V * HI * block + owner), 0
        for rep in range(n_rep):
            low, high = max(begin, share * rep), min(begin + rows, share * (rep + 1))
            if low < high:
                window = min(max(begin - share * rep, 0), share - rows)
                found.append((block, filled, rep, low - share * rep - window, high - low))
                filled += high - low
    return found


def folded(value, used):
    rows, lanes = value.shape
    whole, rest = lanes // LANES, lanes % LANES
    fold = LANES // rest
    deep = rows // fold
    left = value[:, whole * LANES :]
    side = [left[n * deep : (n + 1) * deep] for n in range(fold)]
    if fold * rest < LANES:
        side.append(jnp.zeros((deep, LANES - fold * rest), value.dtype))
    packed = [value[:, n * LANES : (n + 1) * LANES] for n in range(whole)]
    packed.append(jnp.concatenate(side, axis=1))
    if used > whole * rows + deep:
        packed.append(jnp.zeros((used - whole * rows - deep, LANES), value.dtype))
    return jnp.concatenate(packed, axis=0)


def unfolded(packed, rows, lanes):
    whole, rest = lanes // LANES, lanes % LANES
    fold = LANES // rest
    left = packed[whole * rows : whole * rows + rows // fold]
    left = jnp.concatenate([left[:, n * rest : (n + 1) * rest] for n in range(fold)], axis=0)
    return jnp.concatenate([packed[n * rows : (n + 1) * rows] for n in range(whole)] + [left], axis=1)


def fold_size(rows, lanes):
    return -(-(lanes // LANES * rows + rows // (LANES // (lanes % LANES))) // 8) * 8


def pack(*refs):
    out_ref = refs[-1]
    for side in range(HI):
        for duo in range(DUO):
            packed = folded(refs[side][duo].astype(F32), out_ref.shape[2])
            out_ref[duo, side] = packed.astype(BF16)


def multiply(where_ref, here_ref, below_ref, above_ref, first_ref, out_ref, window_ref, second_ref):
    n_rep = window_ref.shape[0]
    rows, depth = second_ref.shape[1:]
    share = first_ref.shape[1]
    for place, ref in enumerate((here_ref, below_ref, above_ref)):
        for duo in range(DUO):
            window_ref[DUO * where_ref[1 + place] + duo] = unfolded(
                ref[duo].astype(F32), rows, depth
            ).astype(BF16)
    for owner in range(V * HI):

        @pl.when(where_ref[0] == owner)
        def _():
            for block, row, rep, held, count in pieces_of(owner, rows, share, n_rep):
                second_ref[block, row : row + count] = window_ref[rep, held : held + count]

    for block in range(second_ref.shape[0]):
        for duo in range(DUO):
            got = lax.dot_general(
                second_ref[block], first_ref[duo], (((1,), (1,)), ((), ())),
                preferred_element_type=F32,
            )
            out_ref[block * DUO + duo] = folded(got, out_ref.shape[1]).astype(BF16)


def unpack(packed_ref, out_ref):
    n_rep, rows = packed_ref.shape[0], out_ref.shape[0]
    share = out_ref.shape[1] // n_rep
    columns = [unfolded(packed_ref[rep].astype(F32), rows, share) for rep in range(n_rep)]
    out_ref[...] = jnp.concatenate(columns, axis=1).astype(BF16)


def body(stem_slabs, site_first, site_second, environment):
    slices, rows, width = stem_slabs.shape
    share = site_first.shape[1]
    n_rep = PAIRS * DUO
    u, v, hi, rep, pair, duo = (lax.axis_index(a) for a in ("u", "v", "hi", REP, *REP))
    vmem = pl.BlockSpec(memory_space=pltpu.VMEM)
    params = pltpu.CompilerParams(vmem_limit_bytes=12 << 20)

    first = jnp.einsum(
        "cil,cjl->cij", site_first, stem_slabs, preferred_element_type=F32
    ).astype(BF16)
    even, odd = pick(first, duo), pick(first, 1 - duo)

    depth = V * HI * rows
    windows = []
    for side in range(HI):
        owner = HI * v + side
        block = lax.div(share * rep + (V * HI - 1) * rows - rows * owner, V * HI * rows)
        at = jnp.clip(rows * (owner + V * HI * block) - share * rep, 0, share - rows)
        windows.append(lax.dynamic_slice(site_second, (0, at, depth * u), (slices, rows, depth)))
    windows = pl.pallas_call(
        pack,
        out_shape=jax.ShapeDtypeStruct((DUO, HI, fold_size(rows, depth), LANES), BF16),
        in_specs=[vmem, vmem],
        out_specs=vmem,
        compiler_params=params,
    )(*windows)
    kept = pick(windows, duo)
    taken = lax.ppermute(pick(windows, 1 - duo), "duo", SWAP)
    windows = jnp.stack(
        [jnp.where(duo == 0, kept, taken), jnp.where(duo == 0, taken, kept)], axis=1
    )
    where = [HI * v + hi, pair, (pair + PAIRS - 1) % PAIRS, (pair + 1) % PAIRS]

    near = lax.ppermute(odd, "duo", SWAP)
    own = jnp.concatenate(
        [jnp.where(duo == 0, even, near), jnp.where(duo == 0, near, even)], axis=0
    )
    other = lax.ppermute(own, "hi", SWAP)
    ring = HI * n_rep
    up = jnp.where(pair < PAIRS - 1, hi, 1 - hi)
    down = jnp.where(pair > 0, hi, 1 - hi)
    turn = [(i, (i + DUO) % ring) for i in range(ring)]
    below = lax.ppermute(pick(windows, up), Z, turn)
    above = lax.ppermute(pick(windows, down), Z, [(j, i) for i, j in turn])
    beside = [lax.ppermute(own, "v", SWAP), lax.ppermute(other, "v", SWAP)]
    ours, theirs = (
        jnp.concatenate([jnp.where(hi == 0, a, b), jnp.where(hi == 0, b, a)], axis=1)
        for a, b in ((own, other), beside)
    )
    first = jnp.concatenate(
        [jnp.where(v == 0, ours, theirs), jnp.where(v == 0, theirs, ours)], axis=1
    ).reshape(DUO, share, depth)

    deep = fold_size(rows, share)
    part = pl.pallas_call(
        multiply,
        out_shape=jax.ShapeDtypeStruct((U * DUO, deep, LANES), BF16),
        in_specs=[pl.BlockSpec(memory_space=pltpu.SMEM), vmem, vmem, vmem, vmem],
        out_specs=vmem,
        scratch_shapes=[
            pltpu.VMEM((n_rep, rows, depth), BF16),
            pltpu.VMEM((U, rows, depth), BF16),
        ],
        compiler_params=params,
    )(jnp.stack(where).astype(jnp.int32), pick(windows, hi), below, above, first)
    part = lax.all_to_all(part, ("u", "duo"), 0, 0, tiled=True)
    part = part.reshape(U, DUO, deep, LANES).astype(F32).sum(0)
    weights = environment.astype(F32)[:, :, None, None]
    terms = sum(weights[c] * part[c] for c in range(slices)).astype(BF16)
    terms = lax.all_to_all(terms, ("x", "core"), 0, 0, tiled=True)
    closed = jnp.sum(terms.astype(F32), 0).astype(BF16)
    whole = spread(closed, REP, n_rep)
    return pl.pallas_call(
        unpack,
        out_shape=jax.ShapeDtypeStruct((rows, width), BF16),
        in_specs=[vmem],
        out_specs=vmem,
        compiler_params=params,
    )(whole)[None]


def solution(mesh):
    fine = Mesh(
        mesh.devices.reshape(4, 2, U, V, HI, PAIRS, DUO),
        ("x", "core", "u", "v", "hi", *REP),
    )
    cuts, stem = ("x", "core"), ("u", "v", "hi")
    placed = (P(cuts, stem, None), P(cuts, REP, None), P(cuts, REP, None), P(cuts, None))
    return jax.shard_map(
        body, mesh=fine, in_specs=placed, out_specs=P(cuts, stem, None), check_vma=False
    )
```

```python
import jax
import jax.numpy as jnp
from jax import lax
from jax.experimental import pallas as pl
from jax.experimental.pallas import tpu as pltpu
from jax.sharding import Mesh, PartitionSpec as P


X, CORE, U, V, HI, PAIRS, DUO = 4, 2, 4, 2, 2, 3, 2
LANES = 128
SWAP = [(0, 1), (1, 0)]
REP = ("pair", "duo")
Z = ("hi", *REP)
F32, BF16 = jnp.float32, jnp.bfloat16


def spread(block, axis, n):
    return lax.all_to_all(
        jnp.broadcast_to(block[None], (n, *block.shape)), axis, 0, 0, tiled=True
    )


def pick(array, index):
    return lax.dynamic_index_in_dim(array, index, 0, keepdims=False)


def pieces_of(owner, rows, share, n_rep):
    found = []
    for block in range(U):
        begin, filled = rows * (V * HI * block + owner), 0
        for rep in range(n_rep):
            low, high = max(begin, share * rep), min(begin + rows, share * (rep + 1))
            if low < high:
                window = min(max(begin - share * rep, 0), share - rows)
                found.append((block, filled, rep, low - share * rep - window, high - low))
                filled += high - low
    return found


def folded(value, used):
    rows, lanes = value.shape
    whole, rest = lanes // LANES, lanes % LANES
    fold = LANES // rest
    deep = rows // fold
    left = value[:, whole * LANES :]
    side = [left[n * deep : (n + 1) * deep] for n in range(fold)]
    if fold * rest < LANES:
        side.append(jnp.zeros((deep, LANES - fold * rest), value.dtype))
    packed = [value[:, n * LANES : (n + 1) * LANES] for n in range(whole)]
    packed.append(jnp.concatenate(side, axis=1))
    if used > whole * rows + deep:
        packed.append(jnp.zeros((used - whole * rows - deep, LANES), value.dtype))
    return jnp.concatenate(packed, axis=0)


def unfolded(packed, rows, lanes):
    whole, rest = lanes // LANES, lanes % LANES
    fold = LANES // rest
    left = packed[whole * rows : whole * rows + rows // fold]
    left = jnp.concatenate([left[:, n * rest : (n + 1) * rest] for n in range(fold)], axis=0)
    return jnp.concatenate([packed[n * rows : (n + 1) * rows] for n in range(whole)] + [left], axis=1)


def fold_size(rows, lanes):
    return -(-(lanes // LANES * rows + rows // (LANES // (lanes % LANES))) // 8) * 8


def pack(*refs):
    out_ref = refs[-1]
    for side in range(HI):
        for duo in range(DUO):
            packed = folded(refs[side][duo].astype(F32), out_ref.shape[2])
            out_ref[duo, side] = packed.astype(BF16)


def multiply(where_ref, here_ref, below_ref, above_ref, first_ref, out_ref, window_ref, second_ref):
    n_rep = window_ref.shape[0]
    rows, depth = second_ref.shape[1:]
    share = first_ref.shape[1]
    for place, ref in enumerate((here_ref, below_ref, above_ref)):
        for duo in range(DUO):
            window_ref[DUO * where_ref[1 + place] + duo] = unfolded(
                ref[duo].astype(F32), rows, depth
            ).astype(BF16)
    for owner in range(V * HI):

        @pl.when(where_ref[0] == owner)
        def _():
            for block, row, rep, held, count in pieces_of(owner, rows, share, n_rep):
                second_ref[block, row : row + count] = window_ref[rep, held : held + count]

    for block in range(second_ref.shape[0]):
        for duo in range(DUO):
            got = lax.dot_general(
                second_ref[block], first_ref[duo], (((1,), (1,)), ((), ())),
                preferred_element_type=F32,
            )
            out_ref[duo * U + block] = folded(got, out_ref.shape[1]).astype(BF16)


def unpack(packed_ref, out_ref):
    n_rep, rows = packed_ref.shape[0], out_ref.shape[0]
    share = out_ref.shape[1] // n_rep
    columns = [
        unfolded(packed_ref[duo * PAIRS + pair].astype(F32), rows, share)
        for pair in range(PAIRS)
        for duo in range(DUO)
    ]
    out_ref[...] = jnp.concatenate(columns, axis=1).astype(BF16)


def body(stem_slabs, site_first, site_second, environment):
    slices, rows, width = stem_slabs.shape
    share = site_first.shape[1]
    n_rep = PAIRS * DUO
    u, v, hi, rep, pair, duo = (lax.axis_index(a) for a in ("u", "v", "hi", REP, *REP))
    vmem = pl.BlockSpec(memory_space=pltpu.VMEM)
    params = pltpu.CompilerParams(vmem_limit_bytes=12 << 20)

    first = jnp.einsum(
        "cil,cjl->cij", site_first, stem_slabs, preferred_element_type=F32
    ).astype(BF16)
    even, odd = pick(first, duo), pick(first, 1 - duo)

    depth = V * HI * rows
    windows = []
    for side in range(HI):
        owner = HI * v + side
        block = lax.div(share * rep + (V * HI - 1) * rows - rows * owner, V * HI * rows)
        at = jnp.clip(rows * (owner + V * HI * block) - share * rep, 0, share - rows)
        windows.append(lax.dynamic_slice(site_second, (0, at, depth * u), (slices, rows, depth)))
    windows = pl.pallas_call(
        pack,
        out_shape=jax.ShapeDtypeStruct((DUO, HI, fold_size(rows, depth), LANES), BF16),
        in_specs=[vmem, vmem],
        out_specs=vmem,
        compiler_params=params,
    )(*windows)
    kept = pick(windows, duo)
    taken = lax.ppermute(pick(windows, 1 - duo), "duo", SWAP)
    windows = jnp.stack(
        [jnp.where(duo == 0, kept, taken), jnp.where(duo == 0, taken, kept)], axis=1
    )
    where = [HI * v + hi, pair, (pair + PAIRS - 1) % PAIRS, (pair + 1) % PAIRS]

    near = lax.ppermute(odd, "duo", SWAP)
    own = jnp.concatenate(
        [jnp.where(duo == 0, even, near), jnp.where(duo == 0, near, even)], axis=0
    )
    other = lax.ppermute(own, "hi", SWAP)
    ring = HI * n_rep
    up = jnp.where(pair < PAIRS - 1, hi, 1 - hi)
    down = jnp.where(pair > 0, hi, 1 - hi)
    turn = [(i, (i + DUO) % ring) for i in range(ring)]
    below = lax.ppermute(pick(windows, up), Z, turn)
    above = lax.ppermute(pick(windows, down), Z, [(j, i) for i, j in turn])
    beside = [lax.ppermute(own, "v", SWAP), lax.ppermute(other, "v", SWAP)]
    ours, theirs = (
        jnp.concatenate([jnp.where(hi == 0, a, b), jnp.where(hi == 0, b, a)], axis=1)
        for a, b in ((own, other), beside)
    )
    first = jnp.concatenate(
        [jnp.where(v == 0, ours, theirs), jnp.where(v == 0, theirs, ours)], axis=1
    ).reshape(DUO, share, depth)

    deep = fold_size(rows, share)
    part = pl.pallas_call(
        multiply,
        out_shape=jax.ShapeDtypeStruct((U * DUO, deep, LANES), BF16),
        in_specs=[pl.BlockSpec(memory_space=pltpu.SMEM), vmem, vmem, vmem, vmem],
        out_specs=vmem,
        scratch_shapes=[
            pltpu.VMEM((n_rep, rows, depth), BF16),
            pltpu.VMEM((U, rows, depth), BF16),
        ],
        compiler_params=params,
    )(jnp.stack(where).astype(jnp.int32), pick(windows, hi), below, above, first)
    part = lax.all_to_all(part, ("duo", "u"), 0, 0, tiled=True)
    part = part.reshape(DUO, U, deep, LANES).astype(F32).sum(1)
    weights = environment.astype(F32).reshape(slices, X, CORE).swapaxes(1, 2)
    weights = weights.reshape(slices, X * CORE, 1, 1)
    terms = sum(weights[c] * part[c] for c in range(slices)).astype(BF16)
    terms = lax.all_to_all(terms, ("core", "x"), 0, 0, tiled=True)
    closed = jnp.sum(terms.astype(F32), 0).astype(BF16)
    whole = spread(closed, REP[::-1], n_rep)
    return pl.pallas_call(
        unpack,
        out_shape=jax.ShapeDtypeStruct((rows, width), BF16),
        in_specs=[vmem],
        out_specs=vmem,
        compiler_params=params,
    )(whole)[None]


def solution(mesh):
    fine = Mesh(
        mesh.devices.reshape(X, CORE, U, V, HI, PAIRS, DUO),
        ("x", "core", "u", "v", "hi", *REP),
    )
    cuts, stem = ("x", "core"), ("u", "v", "hi")
    placed = (P(cuts, stem, None), P(cuts, REP, None), P(cuts, REP, None), P(cuts, None))
    return jax.shard_map(
        body, mesh=fine, in_specs=placed, out_specs=P(cuts, stem, None), check_vma=False
    )
```

```python
import jax
import jax.numpy as jnp
from jax import lax
from jax.experimental import pallas as pl
from jax.experimental.pallas import tpu as pltpu
from jax.sharding import Mesh, PartitionSpec as P


X, CORE, U, V, HI, PAIRS, DUO = 4, 2, 4, 2, 2, 3, 2
LANES = 128
SWAP = [(0, 1), (1, 0)]
REP = ("pair", "duo")
Z = ("hi", *REP)
F32, BF16 = jnp.float32, jnp.bfloat16


def spread(block, axis, n):
    return lax.all_to_all(
        jnp.broadcast_to(block[None], (n, *block.shape)), axis, 0, 0, tiled=True
    )


def pick(array, index):
    return lax.dynamic_index_in_dim(array, index, 0, keepdims=False)


def pieces_of(owner, rows, share, n_rep):
    found = []
    for block in range(U):
        begin, filled = rows * (V * HI * block + owner), 0
        for rep in range(n_rep):
            low, high = max(begin, share * rep), min(begin + rows, share * (rep + 1))
            if low < high:
                window = min(max(begin - share * rep, 0), share - rows)
                found.append((block, filled, rep, low - share * rep - window, high - low))
                filled += high - low
    return found


def folded(value, used):
    rows, lanes = value.shape
    whole, rest = lanes // LANES, lanes % LANES
    fold = LANES // rest
    deep = rows // fold
    left = value[:, whole * LANES :]
    side = [left[n * deep : (n + 1) * deep] for n in range(fold)]
    if fold * rest < LANES:
        side.append(jnp.zeros((deep, LANES - fold * rest), value.dtype))
    packed = [value[:, n * LANES : (n + 1) * LANES] for n in range(whole)]
    packed.append(jnp.concatenate(side, axis=1))
    if used > whole * rows + deep:
        packed.append(jnp.zeros((used - whole * rows - deep, LANES), value.dtype))
    return jnp.concatenate(packed, axis=0)


def unfolded(packed, rows, lanes):
    whole, rest = lanes // LANES, lanes % LANES
    fold = LANES // rest
    left = packed[whole * rows : whole * rows + rows // fold]
    left = jnp.concatenate([left[:, n * rest : (n + 1) * rest] for n in range(fold)], axis=0)
    return jnp.concatenate([packed[n * rows : (n + 1) * rows] for n in range(whole)] + [left], axis=1)


def fold_size(rows, lanes):
    return -(-(lanes // LANES * rows + rows // (LANES // (lanes % LANES))) // 8) * 8


def pack(duo_ref, low_ref, high_ref, kept_ref, given_ref):
    for side, ref in enumerate((low_ref, high_ref)):
        for out_ref, duo in ((kept_ref, duo_ref[0]), (given_ref, 1 - duo_ref[0])):
            packed = folded(ref[duo].astype(F32), out_ref.shape[1])
            out_ref[side] = packed.astype(BF16)


def multiply(where_ref, here_ref, below_ref, above_ref, first_ref, out_ref, window_ref, second_ref):
    n_rep = window_ref.shape[0]
    rows, depth = second_ref.shape[1:]
    share = first_ref.shape[1]
    for place, ref in enumerate((here_ref, below_ref, above_ref)):
        for duo in range(DUO):
            window_ref[DUO * where_ref[1 + place] + duo] = unfolded(
                ref[duo].astype(F32), rows, depth
            ).astype(BF16)
    for owner in range(V * HI):

        @pl.when(where_ref[0] == owner)
        def _():
            for block, row, rep, held, count in pieces_of(owner, rows, share, n_rep):
                second_ref[block, row : row + count] = window_ref[rep, held : held + count]

    for block in range(second_ref.shape[0]):
        for duo in range(DUO):
            got = lax.dot_general(
                second_ref[block], first_ref[duo], (((1,), (1,)), ((), ())),
                preferred_element_type=F32,
            )
            out_ref[duo * U + block] = folded(got, out_ref.shape[1]).astype(BF16)


def unpack(packed_ref, out_ref):
    n_rep, rows = packed_ref.shape[0], out_ref.shape[0]
    share = out_ref.shape[1] // n_rep
    columns = [
        unfolded(packed_ref[duo * PAIRS + pair].astype(F32), rows, share)
        for pair in range(PAIRS)
        for duo in range(DUO)
    ]
    out_ref[...] = jnp.concatenate(columns, axis=1).astype(BF16)


def body(stem_slabs, site_first, site_second, environment):
    slices, rows, width = stem_slabs.shape
    share = site_first.shape[1]
    n_rep = PAIRS * DUO
    u, v, hi, rep, pair, duo = (lax.axis_index(a) for a in ("u", "v", "hi", REP, *REP))
    vmem = pl.BlockSpec(memory_space=pltpu.VMEM)
    params = pltpu.CompilerParams(vmem_limit_bytes=12 << 20)

    first = jnp.einsum(
        "cil,cjl->cij", site_first, stem_slabs, preferred_element_type=F32
    ).astype(BF16)
    even, odd = pick(first, duo), pick(first, 1 - duo)

    depth = V * HI * rows
    windows = []
    for side in range(HI):
        owner = HI * v + side
        block = lax.div(share * rep + (V * HI - 1) * rows - rows * owner, V * HI * rows)
        at = jnp.clip(rows * (owner + V * HI * block) - share * rep, 0, share - rows)
        windows.append(lax.dynamic_slice(site_second, (0, at, depth * u), (slices, rows, depth)))
    half = jax.ShapeDtypeStruct((HI, fold_size(rows, depth), LANES), BF16)
    kept, given = pl.pallas_call(
        pack,
        out_shape=(half, half),
        in_specs=[pl.BlockSpec(memory_space=pltpu.SMEM), vmem, vmem],
        out_specs=(vmem, vmem),
        compiler_params=params,
    )(duo[None].astype(jnp.int32), *windows)
    taken = lax.ppermute(given, "duo", SWAP)
    windows = jnp.stack(
        [jnp.where(duo == 0, kept, taken), jnp.where(duo == 0, taken, kept)], axis=1
    )
    where = [HI * v + hi, pair, (pair + PAIRS - 1) % PAIRS, (pair + 1) % PAIRS]

    near = lax.ppermute(odd, "duo", SWAP)
    own = jnp.concatenate(
        [jnp.where(duo == 0, even, near), jnp.where(duo == 0, near, even)], axis=0
    )
    other = lax.ppermute(own, "hi", SWAP)
    ring = HI * n_rep
    up = jnp.where(pair < PAIRS - 1, hi, 1 - hi)
    down = jnp.where(pair > 0, hi, 1 - hi)
    turn = [(i, (i + DUO) % ring) for i in range(ring)]
    below = lax.ppermute(pick(windows, up), Z, turn)
    above = lax.ppermute(pick(windows, down), Z, [(j, i) for i, j in turn])
    beside = [lax.ppermute(own, "v", SWAP), lax.ppermute(other, "v", SWAP)]
    ours, theirs = (
        jnp.concatenate([jnp.where(hi == 0, a, b), jnp.where(hi == 0, b, a)], axis=1)
        for a, b in ((own, other), beside)
    )
    first = jnp.concatenate(
        [jnp.where(v == 0, ours, theirs), jnp.where(v == 0, theirs, ours)], axis=1
    ).reshape(DUO, share, depth)

    deep = fold_size(rows, share)
    part = pl.pallas_call(
        multiply,
        out_shape=jax.ShapeDtypeStruct((U * DUO, deep, LANES), BF16),
        in_specs=[pl.BlockSpec(memory_space=pltpu.SMEM), vmem, vmem, vmem, vmem],
        out_specs=vmem,
        scratch_shapes=[
            pltpu.VMEM((n_rep, rows, depth), BF16),
            pltpu.VMEM((U, rows, depth), BF16),
        ],
        compiler_params=params,
    )(jnp.stack(where).astype(jnp.int32), pick(windows, hi), below, above, first)
    part = lax.all_to_all(part, ("duo", "u"), 0, 0, tiled=True)
    part = part.reshape(DUO, U, deep, LANES).astype(F32).sum(1)
    weights = environment.astype(F32).reshape(slices, X, CORE).swapaxes(1, 2)
    weights = weights.reshape(slices, X * CORE, 1, 1)
    terms = sum(weights[c] * part[c] for c in range(slices)).astype(BF16)
    terms = lax.all_to_all(terms, ("core", "x"), 0, 0, tiled=True)
    closed = jnp.sum(terms.astype(F32), 0).astype(BF16)
    whole = spread(closed, REP[::-1], n_rep)
    return pl.pallas_call(
        unpack,
        out_shape=jax.ShapeDtypeStruct((rows, width), BF16),
        in_specs=[vmem],
        out_specs=vmem,
        compiler_params=params,
    )(whole)[None]


def solution(mesh):
    fine = Mesh(
        mesh.devices.reshape(X, CORE, U, V, HI, PAIRS, DUO),
        ("x", "core", "u", "v", "hi", *REP),
    )
    cuts, stem = ("x", "core"), ("u", "v", "hi")
    placed = (P(cuts, stem, None), P(cuts, REP, None), P(cuts, REP, None), P(cuts, None))
    return jax.shard_map(
        body, mesh=fine, in_specs=placed, out_specs=P(cuts, stem, None), check_vma=False
    )
```

```python
import jax
import jax.numpy as jnp
from jax import lax
from jax.experimental import pallas as pl
from jax.experimental.pallas import tpu as pltpu
from jax.sharding import Mesh, PartitionSpec as P


X, CORE, U, V, HI, PAIRS, DUO = 4, 2, 4, 2, 2, 3, 2
LANES = 128
SWAP = [(0, 1), (1, 0)]
REP = ("pair", "duo")
Z = ("hi", *REP)
F32, BF16 = jnp.float32, jnp.bfloat16


def spread(block, axis, n):
    return lax.all_to_all(
        jnp.broadcast_to(block[None], (n, *block.shape)), axis, 0, 0, tiled=True
    )


def pick(array, index):
    return lax.dynamic_index_in_dim(array, index, 0, keepdims=False)


def pieces_of(owner, rows, share, n_rep):
    found = []
    for block in range(U):
        begin, filled = rows * (V * HI * block + owner), 0
        for rep in range(n_rep):
            low, high = max(begin, share * rep), min(begin + rows, share * (rep + 1))
            if low < high:
                window = min(max(begin - share * rep, 0), share - rows)
                found.append((block, filled, rep, low - share * rep - window, high - low))
                filled += high - low
    return found


def folded(value, used):
    rows, lanes = value.shape
    whole, rest = lanes // LANES, lanes % LANES
    fold = LANES // rest
    deep = rows // fold
    left = value[:, whole * LANES :]
    side = [left[n * deep : (n + 1) * deep] for n in range(fold)]
    if fold * rest < LANES:
        side.append(jnp.zeros((deep, LANES - fold * rest), value.dtype))
    packed = [value[:, n * LANES : (n + 1) * LANES] for n in range(whole)]
    packed.append(jnp.concatenate(side, axis=1))
    if used > whole * rows + deep:
        packed.append(jnp.zeros((used - whole * rows - deep, LANES), value.dtype))
    return jnp.concatenate(packed, axis=0)


def unfolded(packed, rows, lanes):
    whole, rest = lanes // LANES, lanes % LANES
    fold = LANES // rest
    left = packed[whole * rows : whole * rows + rows // fold]
    left = jnp.concatenate([left[:, n * rest : (n + 1) * rest] for n in range(fold)], axis=0)
    return jnp.concatenate([packed[n * rows : (n + 1) * rows] for n in range(whole)] + [left], axis=1)


def fold_size(rows, lanes):
    return -(-(lanes // LANES * rows + rows // (LANES // (lanes % LANES))) // 8) * 8


def pack(duo_ref, low_ref, high_ref, kept_ref, given_ref):
    for side, ref in enumerate((low_ref, high_ref)):
        for out_ref, duo in ((kept_ref, duo_ref[0]), (given_ref, 1 - duo_ref[0])):
            packed = folded(ref[duo].astype(F32), out_ref.shape[1])
            out_ref[side] = packed.astype(BF16)


def assemble(where_ref, here_ref, below_ref, above_ref, second_ref, window_ref):
    n_rep = window_ref.shape[0]
    rows, depth = second_ref.shape[1:]
    share = U * depth // n_rep
    for place, ref in enumerate((here_ref, below_ref, above_ref)):
        for duo in range(DUO):
            window_ref[DUO * where_ref[1 + place] + duo] = unfolded(
                ref[duo].astype(F32), rows, depth
            ).astype(BF16)
    for owner in range(V * HI):

        @pl.when(where_ref[0] == owner)
        def _():
            for block, row, rep, held, count in pieces_of(owner, rows, share, n_rep):
                second_ref[block, row : row + count] = window_ref[rep, held : held + count]


def multiply(second_ref, first_ref, out_ref):
    for block in range(second_ref.shape[0]):
        for duo in range(DUO):
            got = lax.dot_general(
                second_ref[block], first_ref[duo], (((1,), (1,)), ((), ())),
                preferred_element_type=F32,
            )
            out_ref[duo * U + block] = folded(got, out_ref.shape[1]).astype(BF16)


def unpack(packed_ref, out_ref):
    n_rep, rows = packed_ref.shape[0], out_ref.shape[0]
    share = out_ref.shape[1] // n_rep
    columns = [
        unfolded(packed_ref[duo * PAIRS + pair].astype(F32), rows, share)
        for pair in range(PAIRS)
        for duo in range(DUO)
    ]
    out_ref[...] = jnp.concatenate(columns, axis=1).astype(BF16)


def body(stem_slabs, site_first, site_second, environment):
    slices, rows, width = stem_slabs.shape
    share = site_first.shape[1]
    n_rep = PAIRS * DUO
    u, v, hi, rep, pair, duo = (lax.axis_index(a) for a in ("u", "v", "hi", REP, *REP))
    vmem = pl.BlockSpec(memory_space=pltpu.VMEM)
    params = pltpu.CompilerParams(vmem_limit_bytes=12 << 20)

    first = jnp.einsum(
        "cil,cjl->cij", site_first, stem_slabs, preferred_element_type=F32
    ).astype(BF16)
    even, odd = pick(first, duo), pick(first, 1 - duo)

    depth = V * HI * rows
    windows = []
    for side in range(HI):
        owner = HI * v + side
        block = lax.div(share * rep + (V * HI - 1) * rows - rows * owner, V * HI * rows)
        at = jnp.clip(rows * (owner + V * HI * block) - share * rep, 0, share - rows)
        windows.append(lax.dynamic_slice(site_second, (0, at, depth * u), (slices, rows, depth)))
    half = jax.ShapeDtypeStruct((HI, fold_size(rows, depth), LANES), BF16)
    kept, given = pl.pallas_call(
        pack,
        out_shape=(half, half),
        in_specs=[pl.BlockSpec(memory_space=pltpu.SMEM), vmem, vmem],
        out_specs=(vmem, vmem),
        compiler_params=params,
    )(duo[None].astype(jnp.int32), *windows)
    taken = lax.ppermute(given, "duo", SWAP)
    windows = jnp.stack(
        [jnp.where(duo == 0, kept, taken), jnp.where(duo == 0, taken, kept)], axis=1
    )
    where = [HI * v + hi, pair, (pair + PAIRS - 1) % PAIRS, (pair + 1) % PAIRS]

    near = lax.ppermute(odd, "duo", SWAP)
    own = jnp.concatenate(
        [jnp.where(duo == 0, even, near), jnp.where(duo == 0, near, even)], axis=0
    )
    other = lax.ppermute(own, "hi", SWAP)
    ring = HI * n_rep
    up = jnp.where(pair < PAIRS - 1, hi, 1 - hi)
    down = jnp.where(pair > 0, hi, 1 - hi)
    turn = [(i, (i + DUO) % ring) for i in range(ring)]
    below = lax.ppermute(pick(windows, up), Z, turn)
    above = lax.ppermute(pick(windows, down), Z, [(j, i) for i, j in turn])
    beside = [lax.ppermute(own, "v", SWAP), lax.ppermute(other, "v", SWAP)]
    ours, theirs = (
        jnp.concatenate([jnp.where(hi == 0, a, b), jnp.where(hi == 0, b, a)], axis=1)
        for a, b in ((own, other), beside)
    )
    first = jnp.concatenate(
        [jnp.where(v == 0, ours, theirs), jnp.where(v == 0, theirs, ours)], axis=1
    ).reshape(DUO, share, depth)

    deep = fold_size(rows, share)
    second = pl.pallas_call(
        assemble,
        out_shape=jax.ShapeDtypeStruct((U, rows, depth), BF16),
        in_specs=[pl.BlockSpec(memory_space=pltpu.SMEM), vmem, vmem, vmem],
        out_specs=vmem,
        scratch_shapes=[pltpu.VMEM((n_rep, rows, depth), BF16)],
        compiler_params=params,
    )(jnp.stack(where).astype(jnp.int32), pick(windows, hi), below, above)
    part = pl.pallas_call(
        multiply,
        out_shape=jax.ShapeDtypeStruct((U * DUO, deep, LANES), BF16),
        in_specs=[vmem, vmem],
        out_specs=vmem,
        compiler_params=params,
    )(second, first)
    part = lax.all_to_all(part, ("duo", "u"), 0, 0, tiled=True)
    part = part.reshape(DUO, U, deep, LANES).astype(F32).sum(1)
    weights = environment.astype(F32).reshape(slices, X, CORE).swapaxes(1, 2)
    weights = weights.reshape(slices, X * CORE, 1, 1)
    terms = sum(weights[c] * part[c] for c in range(slices)).astype(BF16)
    terms = lax.all_to_all(terms, ("core", "x"), 0, 0, tiled=True)
    closed = jnp.sum(terms.astype(F32), 0).astype(BF16)
    whole = spread(closed, REP[::-1], n_rep)
    return pl.pallas_call(
        unpack,
        out_shape=jax.ShapeDtypeStruct((rows, width), BF16),
        in_specs=[vmem],
        out_specs=vmem,
        compiler_params=params,
    )(whole)[None]


def solution(mesh):
    fine = Mesh(
        mesh.devices.reshape(X, CORE, U, V, HI, PAIRS, DUO),
        ("x", "core", "u", "v", "hi", *REP),
    )
    cuts, stem = ("x", "core"), ("u", "v", "hi")
    placed = (P(cuts, stem, None), P(cuts, REP, None), P(cuts, REP, None), P(cuts, None))
    return jax.shard_map(
        body, mesh=fine, in_specs=placed, out_specs=P(cuts, stem, None), check_vma=False
    )
```
